32 devices in a mesh: task: 8 (over z, x), own: 4 (over y, core).
Axes of the slice: x: 2, y: 2, z: 4, core: 2. Of those that a mesh axis runs over, the one named last changes fastest.
Arguments:
- amplitudes: bfloat16 [64, 384, 128], P(('task', 'own')), may hold values from -6 to 6
- integrals: bfloat16 [2048, 128, 128], P(('task', 'own')), may hold values from -0.125 to 0.125
- task_tiles: int32 [2048, 3], P(('task', 'own')), may hold values from 0 to 7, as said below
- task_count: int32 [32], P(('task', 'own')), may hold values from 8 to 64, as said below
Outputs:
- residual: float32 [64, 384, 128], P(('task', 'own'))
The draws below stay inside these ranges and needn't reach their ends.
Inputs may be any that keep to these rules, and one draw needn't show every extreme that they name: `task_tiles`: column 0 is 0 or 1, columns 1 and 2 are tiles of a group, below 8. Among the slots of one executor, the target tiles t with t // 2 = o number exactly 16 for every o below 4. `task_count`: in every task group one executor has all 64 slots live.
All inputs are finite; a program needn't handle non-finite values.
Results may differ from the reference program's by a relative error of at most 0.0003.
Values may be sent and summed in bfloat16 or wider, within the bound.
A program may use at most 64 MiB of HBM per device.

```python
import jax
import jax.numpy as jnp
from jax import lax

TILE = 128
OCC_PAIRS = 384
TILES_DEV = 2
TASKS_DEV = 64
OWNERS = 4
GROUPS = 8
GROUP_TILES = 8
NT = 64
NK = 2048
EXECUTORS = 32


def draw_task_tiles(key, part):
    keys = jax.random.split(jax.random.fold_in(key, 11), 4)
    offset = jax.random.randint(keys[0], (NK,), 0, 2)
    source = jax.random.randint(keys[1], (NK,), 0, GROUP_TILES)
    base = jnp.repeat(jnp.arange(OWNERS, dtype=jnp.int32), TASKS_DEV // OWNERS)
    shuffle_keys = jax.random.split(keys[2], EXECUTORS)
    owners_of = jax.vmap(lambda k: jax.random.permutation(k, base))(shuffle_keys).reshape(NK)
    within = jax.random.randint(keys[3], (NK,), 0, TILES_DEV)
    target = owners_of * TILES_DEV + within
    return jnp.stack([offset, source, target], 1).astype(jnp.int32)


def draw_task_count(key, part):
    keys = jax.random.split(jax.random.fold_in(key, 23), 2)
    counts = jax.random.randint(keys[0], (EXECUTORS,), TASKS_DEV // 8, TASKS_DEV // 2 + 1)
    fullest = jax.random.randint(keys[1], (GROUPS,), 0, OWNERS)
    where_full = jnp.arange(GROUPS, dtype=jnp.int32) * OWNERS + fullest
    return counts.at[where_full].set(TASKS_DEV).astype(jnp.int32)


def shard_levels(own_key, shape, cuts, smallest, largest):
    factor_of, own = 1.0, jax.random.fold_in(own_key, 6)
    for position, blocks in cuts:
        heights = jnp.exp(jax.random.uniform(jax.random.fold_in(own, position), (blocks,), jnp.float32, smallest / len(cuts), largest / len(cuts)))
        factor_of = factor_of * jnp.repeat(heights, shape[position] // blocks).reshape([-1 if axis == position else 1 for axis in range(len(shape))])
    return factor_of


def centred(key, dims, scale, bound, cuts=(), kind=jnp.bfloat16):
    values = jax.random.normal(key, dims, jnp.float32) * scale
    if len(cuts) > 0:
        values = shard_levels(key, dims, cuts, -0.22, 0.18) * values
    return jnp.clip(values, min=-bound, max=bound).astype(kind)


def setup_inputs(seed: int = 0) -> dict:
    seeds = jax.random.split(jax.random.key(seed), 5)
    return {
        "amplitudes": centred(seeds[0], (NT, OCC_PAIRS, TILE), 1.0, 6.0, ((0, 32),)),
        "integrals": centred(seeds[1], (NK, TILE, TILE), (TILE * 16) ** -0.5, 0.125, ((0, 32),)),
        "task_tiles": draw_task_tiles(jax.random.fold_in(seeds[4], 71), 0),
        "task_count": draw_task_count(jax.random.fold_in(seeds[4], 71), 0),
    }


def reference(amplitudes, integrals, task_tiles, task_count):
    slots = jnp.arange(TASKS_DEV, dtype=jnp.int32)

    def one_executor(total, executor):
        group = executor // OWNERS
        begin = (executor * TASKS_DEV).astype(jnp.int32)
        blocks = lax.dynamic_slice_in_dim(integrals, begin, TASKS_DEV, 0).astype(jnp.float32)
        lists = lax.dynamic_slice_in_dim(task_tiles, begin, TASKS_DEV, 0)
        live = (slots < task_count[executor]).astype(jnp.float32)
        source = (((group - lists[:, 0]) % GROUPS) * GROUP_TILES + lists[:, 1]).astype(jnp.int32)
        target = (group * GROUP_TILES + lists[:, 2]).astype(jnp.int32)
        tiles = amplitudes[source].astype(jnp.float32)
        product = jnp.einsum("kic,kcr->kir", tiles, blocks, precision=lax.Precision.HIGHEST)
        product = product * live[:, None, None]
        return total.at[target].add(product), None

    start = jnp.zeros((NT, OCC_PAIRS, TILE), jnp.float32)
    total, unused = lax.scan(one_executor, start, jnp.arange(EXECUTORS, dtype=jnp.int32))
    return total
```

```python
import functools

import jax
import jax.numpy as jnp
from jax import lax
from jax.experimental import pallas as pl
from jax.experimental.pallas import tpu as pltpu
from jax.sharding import PartitionSpec as P

MESH = pl.DeviceIdType.MESH
CHUNKS = 3
AHEAD = 2
LEVELS = 32767.0
TINY = 1e-33


def kernel(dims, amp, integ, lists, count, out, *scratch):
    groups, n, tiles, slots, rows_all, width = dims
    half = n // 2
    per_owner = slots // n
    rows = rows_all // CHUNKS
    wide = tiles * width
    group_tiles = n * tiles
    gath = scratch[:CHUNKS]
    (vbuf, weights, psend, precv, pown, qsend, qrecv, ssend, srecv, following, source,
     local_sem, v_sem, sy, ry, sn, rn, ss, rs, st, rt, sp, rp, sq, rq, sc, rc) = scratch[CHUNKS:]

    g = lax.axis_index("task")
    me = lax.axis_index("own")
    core = lax.rem(me, 2)
    y = lax.div(me, 2)
    next_g = lax.rem(g + 1, groups)
    prev_g = lax.rem(g + groups - 1, groups)
    sibling = y * 2 + 1 - core
    to_sibling = {"task": g, "own": sibling}
    to_next = {"task": next_g, "own": me}

    def ahead(d):
        return lax.rem(y + d, half) * 2 + core

    def behind(d):
        return lax.rem(y + half - d, half) * 2 + core

    barrier = pltpu.get_barrier_semaphore()
    for d in range(1, half):
        pl.semaphore_signal(barrier, inc=1, device_id={"task": g, "own": ahead(d)}, device_id_type=MESH)
    pl.semaphore_signal(barrier, inc=1, device_id=to_sibling, device_id_type=MESH)
    pl.semaphore_signal(barrier, inc=1, device_id={"task": prev_g, "own": me}, device_id_type=MESH)

    v_copy = pltpu.make_async_copy(integ, vbuf, v_sem)
    v_copy.start()
    local = []

    def own_rows(c):
        return amp.at[:, pl.ds(c * rows, rows), :]

    def slot(c, offset, owner):
        return gath[c].at[pl.ds((offset * n + owner) * tiles, tiles)]

    for c in range(CHUNKS):
        copy = pltpu.make_async_copy(own_rows(c), slot(c, 0, me), local_sem.at[c])
        copy.start()
        local.append(copy)

    sends = []

    def remote(src, dst, send_sem, recv_sem, device):
        copy = pltpu.make_async_remote_copy(
            src_ref=src, dst_ref=dst, send_sem=send_sem, recv_sem=recv_sem, device_id=device, device_id_type=MESH
        )
        copy.start()
        sends.append(copy)

    def arrived(dst, recv_sem):
        pltpu.make_async_copy(dst, dst, recv_sem).wait()

    pl.semaphore_wait(barrier, half + 1)

    def send_y(c):
        for d in range(1, half):
            remote(own_rows(c), slot(c, 0, me), sy.at[c, d - 1], ry.at[c, d - 1], {"task": g, "own": ahead(d)})

    def send_next(c):
        remote(own_rows(c), slot(c, 1, me), sn.at[c, 0], rn.at[c, 0], to_next)

    def send_sibling(c):
        remote(own_rows(c), slot(c, 0, me), ss.at[c, 0], rs.at[c, 0], to_sibling)

    for c in range(CHUNKS):
        send_y(c)
        if c < AHEAD:
            send_next(c)
        send_sibling(c)

    def relay_y(c):
        for d in range(1, half):
            here = slot(c, 0, behind(d))
            arrived(here, ry.at[c, d - 1])
            remote(here, slot(c, 1, behind(d)), sn.at[c, d], rn.at[c, d], to_next)
            remote(here, slot(c, 0, behind(d)), ss.at[c, d], rs.at[c, d], to_sibling)
        if c + AHEAD < CHUNKS:
            send_next(c + AHEAD)

    def relay_next(c):
        for d in range(half):
            here = slot(c, 1, behind(d))
            arrived(here, rn.at[c, d])
            remote(here, slot(c, 1, behind(d)), st.at[c, d], rt.at[c, d], to_sibling)

    for o in range(n):
        following[slots * n + o] = 0

    def back(step, firsts):
        k = slots - 1 - step
        owner = lax.div(lists[k, 2], tiles)
        fresh = []
        for o in range(n):
            first = jnp.where(owner == o, k, firsts[o])
            following[k * n + o] = first
            fresh.append(first)
        return tuple(fresh)

    lax.fori_loop(0, slots, back, tuple(jnp.int32(0) for _ in range(n)))
    v_copy.wait()
    live_slots = count[0]

    def weigh(o, carry):
        k = following[o]
        for j in range(per_owner):
            block = vbuf[k]
            target = lax.rem(lists[k, 2], tiles)
            source[o * per_owner + j] = lists[k, 0] * group_tiles + lists[k, 1]
            for t in range(tiles):
                keep = jnp.logical_and(target == t, k < live_slots)
                weights[o, j * width:(j + 1) * width, t * width:(t + 1) * width] = jnp.where(
                    keep, block, jnp.zeros_like(block)
                )
            k = following[(k + 1) * n + o]
        return carry

    lax.fori_loop(0, n, weigh, 0)

    def product(c, o):
        total = jnp.zeros((rows, wide), jnp.float32)
        for j in range(0, per_owner, 2):
            left = gath[c][source[o * per_owner + j]]
            right = gath[c][source[o * per_owner + j + 1]]
            total = total + jnp.dot(
                jnp.concatenate([left, right], -1),
                weights[o, j * width:(j + 2) * width, :],
                preferred_element_type=jnp.float32,
            )
        return total

    def compute(c):
        local[c].wait()
        for d in range(half):
            other = lax.rem(y + half - d, half) * 2 + 1 - core
            arrived(slot(c, 0, other), rs.at[c, d])
            arrived(slot(c, 1, other), rt.at[c, d])
        for d in range(half):
            psend[c, d] = product(c, lax.rem(y + d + 1, half) * 2 + 1 - core)
            remote(psend.at[c, d], precv.at[c, d], sp.at[c, d], rp.at[c, d], to_sibling)
        for d in range(half):
            pown[c, d] = product(c, lax.rem(y + d + 1, half) * 2 + core)

    def exchange(c):
        for d in range(half - 1):
            arrived(precv.at[c, d], rp.at[c, d])
            total = pown[c, d] + precv[c, d]
            top = jnp.maximum(jnp.max(jnp.abs(total), axis=0, keepdims=True), TINY)
            qsend[c, d] = jnp.round(total * (LEVELS / top)).astype(jnp.int32).astype(jnp.int16)
            ssend[c, d] = jnp.broadcast_to(top * (1.0 / LEVELS), (8, wide))
            device = {"task": g, "own": ahead(d + 1)}
            remote(qsend.at[c, d], qrecv.at[c, d], sq.at[c, d], rq.at[c, d], device)
            remote(ssend.at[c, d], srecv.at[c, d], sc.at[c, d], rc.at[c, d], device)

    def finish(c):
        arrived(precv.at[c, half - 1], rp.at[c, half - 1])
        total = pown[c, half - 1] + precv[c, half - 1]
        for d in range(half - 1):
            arrived(qrecv.at[c, d], rq.at[c, d])
            arrived(srecv.at[c, d], rc.at[c, d])
            total = total + qrecv[c, d].astype(jnp.int32).astype(jnp.float32) * srecv[c, d][0:1]
        for t in range(tiles):
            out[t, c * rows:(c + 1) * rows, :] = total[:, t * width:(t + 1) * width]

    stages = (relay_y, relay_next, compute, exchange, finish)
    for step in range(CHUNKS + len(stages) - 1):
        for late, stage in enumerate(stages):
            if 0 <= step - late < CHUNKS:
                stage(step - late)
    for copy in sends:
        copy.wait_send()


def shards(amplitudes, integrals, task_tiles, task_count):
    tiles, rows_all, width = amplitudes.shape
    slots = integrals.shape[0]
    groups, n = lax.axis_size("task"), lax.axis_size("own")
    half = n // 2
    rows = rows_all // CHUNKS
    wide = tiles * width
    dma = pltpu.SemaphoreType.DMA
    peers = half - 1
    scratch = [pltpu.VMEM((2 * n * tiles, rows, width), amplitudes.dtype) for _ in range(CHUNKS)]
    scratch += [
        pltpu.VMEM(integrals.shape, integrals.dtype),
        pltpu.VMEM((n, slots // n * width, wide), integrals.dtype),
        pltpu.VMEM((CHUNKS, half, rows, wide), jnp.float32),
        pltpu.VMEM((CHUNKS, half, rows, wide), jnp.float32),
        pltpu.VMEM((CHUNKS, half, rows, wide), jnp.float32),
        pltpu.VMEM((CHUNKS, peers, rows, wide), jnp.int16),
        pltpu.VMEM((CHUNKS, peers, rows, wide), jnp.int16),
        pltpu.VMEM((CHUNKS, peers, 8, wide), jnp.float32),
        pltpu.VMEM((CHUNKS, peers, 8, wide), jnp.float32),
        pltpu.SMEM(((slots + 1) * n,), jnp.int32),
        pltpu.SMEM((slots,), jnp.int32),
        dma((CHUNKS,)),
        dma,
        dma((CHUNKS, peers)), dma((CHUNKS, peers)),
        dma((CHUNKS, half)), dma((CHUNKS, half)),
        dma((CHUNKS, half)), dma((CHUNKS, half)),
        dma((CHUNKS, half)), dma((CHUNKS, half)),
        dma((CHUNKS, half)), dma((CHUNKS, half)),
        dma((CHUNKS, peers)), dma((CHUNKS, peers)),
        dma((CHUNKS, peers)), dma((CHUNKS, peers)),
    ]
    dims = (groups, n, tiles, slots, rows_all, width)
    return pl.pallas_call(
        functools.partial(kernel, dims),
        out_shape=jax.ShapeDtypeStruct((tiles, rows_all, width), jnp.float32),
        in_specs=[
            pl.BlockSpec(memory_space=pl.ANY),
            pl.BlockSpec(memory_space=pl.ANY),
            pl.BlockSpec(memory_space=pltpu.SMEM),
            pl.BlockSpec(memory_space=pltpu.SMEM),
        ],
        out_specs=pl.BlockSpec(memory_space=pltpu.VMEM),
        scratch_shapes=scratch,
        compiler_params=pltpu.CompilerParams(collective_id=0, has_side_effects=True),
        name="ladder",
    )(amplitudes, integrals, task_tiles, task_count)


def solution(mesh):
    return jax.shard_map(
        shards,
        mesh=mesh,
        in_specs=(
            P(("task", "own"), None, None),
            P(("task", "own"), None, None),
            P(("task", "own"), None),
            P(("task", "own")),
        ),
        out_specs=P(("task", "own"), None, None),
        check_vma=False,
    )
```

```python
import functools

import jax
import jax.numpy as jnp
from jax import lax
from jax.experimental import pallas as pl
from jax.experimental.pallas import tpu as pltpu
from jax.sharding import PartitionSpec as P

MESH = pl.DeviceIdType.MESH
CHUNKS = 3
AHEAD = 2
LEVELS = 32767.0
TINY = 1e-33


def kernel(dims, amp, integ, lists_hbm, count, out, *scratch):
    groups, n, tiles, slots, rows_all, width = dims
    half = n // 2
    per_owner = slots // n
    rows = rows_all // CHUNKS
    wide = tiles * width
    group_tiles = n * tiles
    gath = scratch[:CHUNKS]
    (vbuf, weights, psend, precv, pown, qsend, qrecv, ssend, srecv, result, lists, following, source,
     local_sem, v_sem, list_sem, out_sem, sy, ry, sn, rn, ss, rs, st, rt, sp, rp, sq, rq, sc, rc) = scratch[CHUNKS:]

    g = lax.axis_index("task")
    me = lax.axis_index("own")
    core = lax.rem(me, 2)
    y = lax.div(me, 2)
    next_g = lax.rem(g + 1, groups)
    prev_g = lax.rem(g + groups - 1, groups)
    sibling = y * 2 + 1 - core
    to_sibling = {"task": g, "own": sibling}
    to_next = {"task": next_g, "own": me}

    def ahead(d):
        return lax.rem(y + d, half) * 2 + core

    def behind(d):
        return lax.rem(y + half - d, half) * 2 + core

    list_copy = pltpu.make_async_copy(lists_hbm, lists, list_sem)
    list_copy.start()
    barrier = pltpu.get_barrier_semaphore()
    for d in range(1, half):
        pl.semaphore_signal(barrier, inc=1, device_id={"task": g, "own": ahead(d)}, device_id_type=MESH)
    pl.semaphore_signal(barrier, inc=1, device_id=to_sibling, device_id_type=MESH)
    pl.semaphore_signal(barrier, inc=1, device_id={"task": prev_g, "own": me}, device_id_type=MESH)

    v_copy = pltpu.make_async_copy(integ, vbuf, v_sem)
    v_copy.start()
    local = []

    def own_rows(c):
        return amp.at[:, pl.ds(c * rows, rows), :]

    def slot(c, offset, owner):
        return gath[c].at[pl.ds((offset * n + owner) * tiles, tiles)]

    for c in range(CHUNKS):
        copy = pltpu.make_async_copy(own_rows(c), slot(c, 0, me), local_sem.at[c])
        copy.start()
        local.append(copy)

    sends, stored = [], []

    def remote(src, dst, send_sem, recv_sem, device):
        copy = pltpu.make_async_remote_copy(
            src_ref=src, dst_ref=dst, send_sem=send_sem, recv_sem=recv_sem, device_id=device, device_id_type=MESH
        )
        copy.start()
        sends.append(copy)

    def arrived(dst, recv_sem):
        pltpu.make_async_copy(dst, dst, recv_sem).wait()

    pl.semaphore_wait(barrier, half + 1)

    def send_y(c):
        for d in range(1, half):
            remote(own_rows(c), slot(c, 0, me), sy.at[c, d - 1], ry.at[c, d - 1], {"task": g, "own": ahead(d)})

    def send_next(c):
        remote(own_rows(c), slot(c, 1, me), sn.at[c, 0], rn.at[c, 0], to_next)

    def send_sibling(c):
        remote(own_rows(c), slot(c, 0, me), ss.at[c, 0], rs.at[c, 0], to_sibling)

    for c in range(CHUNKS):
        send_y(c)
        if c < AHEAD:
            send_next(c)
        send_sibling(c)

    def relay_y(c):
        for d in range(1, half):
            here = slot(c, 0, behind(d))
            arrived(here, ry.at[c, d - 1])
            remote(here, slot(c, 1, behind(d)), sn.at[c, d], rn.at[c, d], to_next)
            remote(here, slot(c, 0, behind(d)), ss.at[c, d], rs.at[c, d], to_sibling)
        if c + AHEAD < CHUNKS:
            send_next(c + AHEAD)

    def relay_next(c):
        for d in range(half):
            here = slot(c, 1, behind(d))
            arrived(here, rn.at[c, d])
            remote(here, slot(c, 1, behind(d)), st.at[c, d], rt.at[c, d], to_sibling)

    list_copy.wait()
    for o in range(n):
        following[slots * n + o] = 0

    def back(step, firsts):
        k = slots - 1 - step
        owner = lax.div(lists[2, k], tiles)
        fresh = []
        for o in range(n):
            first = jnp.where(owner == o, k, firsts[o])
            following[k * n + o] = first
            fresh.append(first)
        return tuple(fresh)

    lax.fori_loop(0, slots, back, tuple(jnp.int32(0) for _ in range(n)))
    v_copy.wait()
    live_slots = count[0]

    def weigh(o, carry):
        k = following[o]
        for j in range(per_owner):
            block = vbuf[k]
            target = lax.rem(lists[2, k], tiles)
            source[o * per_owner + j] = lists[0, k] * group_tiles + lists[1, k]
            for t in range(tiles):
                keep = jnp.logical_and(target == t, k < live_slots)
                weights[o, j * width:(j + 1) * width, t * width:(t + 1) * width] = jnp.where(
                    keep, block, jnp.zeros_like(block)
                )
            k = following[(k + 1) * n + o]
        return carry

    lax.fori_loop(0, n, weigh, 0)

    def product(c, o):
        total = jnp.zeros((rows, wide), jnp.float32)
        for j in range(0, per_owner, 2):
            left = gath[c][source[o * per_owner + j]]
            right = gath[c][source[o * per_owner + j + 1]]
            total = total + jnp.dot(
                jnp.concatenate([left, right], -1),
                weights[o, j * width:(j + 2) * width, :],
                preferred_element_type=jnp.float32,
            )
        return total

    def compute(c):
        local[c].wait()
        for d in range(half):
            other = lax.rem(y + half - d, half) * 2 + 1 - core
            arrived(slot(c, 0, other), rs.at[c, d])
            arrived(slot(c, 1, other), rt.at[c, d])
        for d in range(half):
            psend[c, d] = product(c, lax.rem(y + d + 1, half) * 2 + 1 - core)
            remote(psend.at[c, d], precv.at[c, d], sp.at[c, d], rp.at[c, d], to_sibling)
        for d in range(half):
            pown[c, d] = product(c, lax.rem(y + d + 1, half) * 2 + core)

    def exchange(c):
        for d in range(half - 1):
            arrived(precv.at[c, d], rp.at[c, d])
            total = pown[c, d] + precv[c, d]
            top = jnp.maximum(jnp.max(jnp.abs(total), axis=0, keepdims=True), TINY)
            qsend[c, d] = jnp.round(total * (LEVELS / top)).astype(jnp.int32).astype(jnp.int16)
            ssend[c, d] = jnp.broadcast_to(top * (1.0 / LEVELS), (8, wide))
            device = {"task": g, "own": ahead(d + 1)}
            remote(qsend.at[c, d], qrecv.at[c, d], sq.at[c, d], rq.at[c, d], device)
            remote(ssend.at[c, d], srecv.at[c, d], sc.at[c, d], rc.at[c, d], device)

    def finish(c):
        arrived(precv.at[c, half - 1], rp.at[c, half - 1])
        total = pown[c, half - 1] + precv[c, half - 1]
        for d in range(half - 1):
            arrived(qrecv.at[c, d], rq.at[c, d])
            arrived(srecv.at[c, d], rc.at[c, d])
            total = total + qrecv[c, d].astype(jnp.int32).astype(jnp.float32) * srecv[c, d][0:1]
        for t in range(tiles):
            result[t, c * rows:(c + 1) * rows, :] = total[:, t * width:(t + 1) * width]
        done = pl.ds(c * rows, rows)
        copy = pltpu.make_async_copy(result.at[:, done, :], out.at[:, done, :], out_sem.at[c])
        copy.start()
        stored.append(copy)

    stages = (relay_y, relay_next, compute, exchange, finish)
    for step in range(CHUNKS + len(stages) - 1):
        for late, stage in enumerate(stages):
            if 0 <= step - late < CHUNKS:
                stage(step - late)
    for copy in sends:
        copy.wait_send()
    for copy in stored:
        copy.wait()


def shards(amplitudes, integrals, task_tiles, task_count):
    tiles, rows_all, width = amplitudes.shape
    slots = integrals.shape[0]
    groups, n = lax.axis_size("task"), lax.axis_size("own")
    half = n // 2
    rows = rows_all // CHUNKS
    wide = tiles * width
    dma = pltpu.SemaphoreType.DMA
    peers = half - 1
    scratch = [pltpu.VMEM((2 * n * tiles, rows, width), amplitudes.dtype) for _ in range(CHUNKS)]
    scratch += [
        pltpu.VMEM(integrals.shape, integrals.dtype),
        pltpu.VMEM((n, slots // n * width, wide), integrals.dtype),
        pltpu.VMEM((CHUNKS, half, rows, wide), jnp.float32),
        pltpu.VMEM((CHUNKS, half, rows, wide), jnp.float32),
        pltpu.VMEM((CHUNKS, half, rows, wide), jnp.float32),
        pltpu.VMEM((CHUNKS, peers, rows, wide), jnp.int16),
        pltpu.VMEM((CHUNKS, peers, rows, wide), jnp.int16),
        pltpu.VMEM((CHUNKS, peers, 8, wide), jnp.float32),
        pltpu.VMEM((CHUNKS, peers, 8, wide), jnp.float32),
        pltpu.VMEM((tiles, rows_all, width), jnp.float32),
        pltpu.SMEM((3, slots), jnp.int32),
        pltpu.SMEM(((slots + 1) * n,), jnp.int32),
        pltpu.SMEM((slots,), jnp.int32),
        dma((CHUNKS,)),
        dma,
        dma,
        dma((CHUNKS,)),
        dma((CHUNKS, peers)), dma((CHUNKS, peers)),
        dma((CHUNKS, half)), dma((CHUNKS, half)),
        dma((CHUNKS, half)), dma((CHUNKS, half)),
        dma((CHUNKS, half)), dma((CHUNKS, half)),
        dma((CHUNKS, half)), dma((CHUNKS, half)),
        dma((CHUNKS, peers)), dma((CHUNKS, peers)),
        dma((CHUNKS, peers)), dma((CHUNKS, peers)),
    ]
    dims = (groups, n, tiles, slots, rows_all, width)
    return pl.pallas_call(
        functools.partial(kernel, dims),
        out_shape=jax.ShapeDtypeStruct((tiles, rows_all, width), jnp.float32),
        in_specs=[
            pl.BlockSpec(memory_space=pl.ANY),
            pl.BlockSpec(memory_space=pl.ANY),
            pl.BlockSpec(memory_space=pl.ANY),
            pl.BlockSpec(memory_space=pltpu.SMEM),
        ],
        out_specs=pl.BlockSpec(memory_space=pl.ANY),
        scratch_shapes=scratch,
        compiler_params=pltpu.CompilerParams(collective_id=0, has_side_effects=True),
        name="ladder",
    )(amplitudes, integrals, task_tiles.T, task_count)


def solution(mesh):
    return jax.shard_map(
        shards,
        mesh=mesh,
        in_specs=(
            P(("task", "own"), None, None),
            P(("task", "own"), None, None),
            P(("task", "own"), None),
            P(("task", "own")),
        ),
        out_specs=P(("task", "own"), None, None),
        check_vma=False,
    )
```

```python
import functools

import jax
import jax.numpy as jnp
from jax import lax
from jax.experimental import pallas as pl
from jax.experimental.pallas import tpu as pltpu
from jax.sharding import PartitionSpec as P

MESH = pl.DeviceIdType.MESH
SHARES = (8, 8, 8)
VIA_Y = (0, 1)
AHEAD = 2
ORDER = "Y0 N0 Y1 N1 Y2 M0 K0 M1 X0 K1 N2 X1 K2 X2 F0 F1 F2"
LEVELS = 32767.0
TINY = 1e-33


def row_chunks(rows_all):
    sizes = [share * rows_all // sum(SHARES) for share in SHARES]
    return [(sum(sizes[:c]), size) for c, size in enumerate(sizes)]


def kernel(dims, amp, integ, lists_hbm, count, out, *scratch):
    groups, n, tiles, slots, rows_all, width = dims
    half = n // 2
    per_owner = slots // n
    chunks = row_chunks(rows_all)
    CHUNKS = len(chunks)
    wide = tiles * width
    group_tiles = n * tiles
    gath = scratch[:CHUNKS]
    (vbuf, weights, psend, precv, pown, qsend, qrecv, ssend, srecv, result, lists, following, source,
     local_sem, v_sem, list_sem, out_sem, sy, ry, sn, rn, ss, rs, st, rt, sv, rv, sp, rp, sq, rq, sc, rc) = scratch[CHUNKS:]

    g = lax.axis_index("task")
    me = lax.axis_index("own")
    core = lax.rem(me, 2)
    y = lax.div(me, 2)
    next_g = lax.rem(g + 1, groups)
    prev_g = lax.rem(g + groups - 1, groups)
    sibling = y * 2 + 1 - core
    to_sibling = {"task": g, "own": sibling}
    to_next = {"task": next_g, "own": me}

    def ahead(d):
        return lax.rem(y + d, half) * 2 + core

    def behind(d):
        return lax.rem(y + half - d, half) * 2 + core

    list_copy = pltpu.make_async_copy(lists_hbm, lists, list_sem)
    list_copy.start()
    barrier = pltpu.get_barrier_semaphore()
    for d in range(1, half):
        pl.semaphore_signal(barrier, inc=1, device_id={"task": g, "own": ahead(d)}, device_id_type=MESH)
    pl.semaphore_signal(barrier, inc=1, device_id=to_sibling, device_id_type=MESH)
    pl.semaphore_signal(barrier, inc=1, device_id={"task": prev_g, "own": me}, device_id_type=MESH)

    v_copy = pltpu.make_async_copy(integ, vbuf, v_sem)
    v_copy.start()
    local = []

    def own_rows(c):
        return amp.at[:, pl.ds(*chunks[c]), :]

    def slot(c, offset, owner):
        return gath[c].at[pl.ds((offset * n + owner) * tiles, tiles)]

    for c in range(CHUNKS):
        copy = pltpu.make_async_copy(own_rows(c), slot(c, 0, me), local_sem.at[c])
        copy.start()
        local.append(copy)

    sends, stored = [], []

    def remote(src, dst, send_sem, recv_sem, device):
        copy = pltpu.make_async_remote_copy(
            src_ref=src, dst_ref=dst, send_sem=send_sem, recv_sem=recv_sem, device_id=device, device_id_type=MESH
        )
        copy.start()
        sends.append(copy)

    def arrived(dst, recv_sem):
        pltpu.make_async_copy(dst, dst, recv_sem).wait()

    pl.semaphore_wait(barrier, half + 1)

    def send_y(c):
        for d in range(1, half):
            remote(own_rows(c), slot(c, 0, me), sy.at[c, d - 1], ry.at[c, d - 1], {"task": g, "own": ahead(d)})

    def send_next(c):
        remote(own_rows(c), slot(c, 1, me), sn.at[c, 0], rn.at[c, 0], to_next)

    def send_sibling(c):
        remote(own_rows(c), slot(c, 0, me), ss.at[c, 0], rs.at[c, 0], to_sibling)

    for c in range(CHUNKS):
        send_y(c)
        if c < AHEAD:
            send_next(c)
        send_sibling(c)

    def relay_y(c):
        for d in range(1, half):
            here = slot(c, 0, behind(d))
            arrived(here, ry.at[c, d - 1])
            if c not in VIA_Y:
                remote(here, slot(c, 1, behind(d)), sn.at[c, d], rn.at[c, d], to_next)
            remote(here, slot(c, 0, behind(d)), ss.at[c, d], rs.at[c, d], to_sibling)
        if c + AHEAD < CHUNKS:
            send_next(c + AHEAD)

    def relay_next(c):
        for d in range(1 if c in VIA_Y else half):
            here = slot(c, 1, behind(d))
            arrived(here, rn.at[c, d])
            if c in VIA_Y:
                for far in range(1, half):
                    remote(here, here, sv.at[c, far - 1], rv.at[c, far - 1], {"task": g, "own": ahead(far)})
            remote(here, here, st.at[c, d], rt.at[c, d], to_sibling)

    def relay_across(c):
        for d in range(1, half):
            here = slot(c, 1, behind(d))
            arrived(here, rv.at[c, d - 1])
            remote(here, here, st.at[c, d], rt.at[c, d], to_sibling)

    list_copy.wait()
    for o in range(n):
        following[slots * n + o] = 0

    def back(step, firsts):
        k = slots - 1 - step
        owner = lax.div(lists[2, k], tiles)
        fresh = []
        for o in range(n):
            first = jnp.where(owner == o, k, firsts[o])
            following[k * n + o] = first
            fresh.append(first)
        return tuple(fresh)

    lax.fori_loop(0, slots, back, tuple(jnp.int32(0) for _ in range(n)))
    v_copy.wait()
    live_slots = count[0]

    def weigh(o, carry):
        k = following[o]
        for j in range(per_owner):
            block = vbuf[k]
            target = lax.rem(lists[2, k], tiles)
            source[o * per_owner + j] = lists[0, k] * group_tiles + lists[1, k]
            for t in range(tiles):
                keep = jnp.logical_and(target == t, k < live_slots)
                weights[o, j * width:(j + 1) * width, t * width:(t + 1) * width] = jnp.where(
                    keep, block, jnp.zeros_like(block)
                )
            k = following[(k + 1) * n + o]
        return carry

    lax.fori_loop(0, n, weigh, 0)

    def product(c, o):
        total = jnp.zeros((chunks[c][1], wide), jnp.float32)
        for j in range(0, per_owner, 2):
            left = gath[c][source[o * per_owner + j]]
            right = gath[c][source[o * per_owner + j + 1]]
            total = total + jnp.dot(
                jnp.concatenate([left, right], -1),
                weights[o, j * width:(j + 2) * width, :],
                preferred_element_type=jnp.float32,
            )
        return total

    def compute(c):
        local[c].wait()
        for d in range(half):
            other = lax.rem(y + half - d, half) * 2 + 1 - core
            arrived(slot(c, 0, other), rs.at[c, d])
            arrived(slot(c, 1, other), rt.at[c, d])
        for d in range(half):
            mine = pl.ds(*chunks[c])
            psend[d, mine, :] = product(c, lax.rem(y + d + 1, half) * 2 + 1 - core)
            remote(psend.at[d, mine], precv.at[d, mine], sp.at[c, d], rp.at[c, d], to_sibling)
        for d in range(half):
            pown[d, mine, :] = product(c, lax.rem(y + d + 1, half) * 2 + core)

    def exchange(c):
        mine = pl.ds(*chunks[c])
        for d in range(half - 1):
            arrived(precv.at[d, mine], rp.at[c, d])
            total = pown[d, mine, :] + precv[d, mine, :]
            top = jnp.maximum(jnp.max(jnp.abs(total), axis=0, keepdims=True), TINY)
            qsend[d, mine, :] = jnp.round(total * (LEVELS / top)).astype(jnp.int32).astype(jnp.int16)
            ssend[c, d] = jnp.broadcast_to(top * (1.0 / LEVELS), (8, wide))
            device = {"task": g, "own": ahead(d + 1)}
            remote(qsend.at[d, mine], qrecv.at[d, mine], sq.at[c, d], rq.at[c, d], device)
            remote(ssend.at[c, d], srecv.at[c, d], sc.at[c, d], rc.at[c, d], device)

    def finish(c):
        mine = pl.ds(*chunks[c])
        arrived(precv.at[half - 1, mine], rp.at[c, half - 1])
        total = pown[half - 1, mine, :] + precv[half - 1, mine, :]
        for d in range(half - 1):
            arrived(qrecv.at[d, mine], rq.at[c, d])
            arrived(srecv.at[c, d], rc.at[c, d])
            total = total + qrecv[d, mine, :].astype(jnp.int32).astype(jnp.float32) * srecv[c, d][0:1]
        for t in range(tiles):
            result[t, mine, :] = total[:, t * width:(t + 1) * width]
        copy = pltpu.make_async_copy(result.at[:, mine, :], out.at[:, mine, :], out_sem.at[c])
        copy.start()
        stored.append(copy)

    stages = {"Y": relay_y, "N": relay_next, "M": relay_across, "K": compute, "X": exchange, "F": finish}
    for word in ORDER.split():
        stages[word[0]](int(word[1:]))
    for copy in sends:
        copy.wait_send()
    for copy in stored:
        copy.wait()


def shards(amplitudes, integrals, task_tiles, task_count):
    tiles, rows_all, width = amplitudes.shape
    slots = integrals.shape[0]
    groups, n = lax.axis_size("task"), lax.axis_size("own")
    half = n // 2
    chunks = row_chunks(rows_all)
    CHUNKS = len(chunks)
    wide = tiles * width
    dma = pltpu.SemaphoreType.DMA
    peers = half - 1
    scratch = [pltpu.VMEM((2 * n * tiles, size, width), amplitudes.dtype) for _, size in chunks]
    scratch += [
        pltpu.VMEM(integrals.shape, integrals.dtype),
        pltpu.VMEM((n, slots // n * width, wide), integrals.dtype),
        pltpu.VMEM((half, rows_all, wide), jnp.float32),
        pltpu.VMEM((half, rows_all, wide), jnp.float32),
        pltpu.VMEM((half, rows_all, wide), jnp.float32),
        pltpu.VMEM((peers, rows_all, wide), jnp.int16),
        pltpu.VMEM((peers, rows_all, wide), jnp.int16),
        pltpu.VMEM((CHUNKS, peers, 8, wide), jnp.float32),
        pltpu.VMEM((CHUNKS, peers, 8, wide), jnp.float32),
        pltpu.VMEM((tiles, rows_all, width), jnp.float32),
        pltpu.SMEM((3, slots), jnp.int32),
        pltpu.SMEM(((slots + 1) * n,), jnp.int32),
        pltpu.SMEM((slots,), jnp.int32),
        dma((CHUNKS,)),
        dma,
        dma,
        dma((CHUNKS,)),
        dma((CHUNKS, peers)), dma((CHUNKS, peers)),
        dma((CHUNKS, half)), dma((CHUNKS, half)),
        dma((CHUNKS, half)), dma((CHUNKS, half)),
        dma((CHUNKS, half)), dma((CHUNKS, half)),
        dma((CHUNKS, peers)), dma((CHUNKS, peers)),
        dma((CHUNKS, half)), dma((CHUNKS, half)),
        dma((CHUNKS, peers)), dma((CHUNKS, peers)),
        dma((CHUNKS, peers)), dma((CHUNKS, peers)),
    ]
    dims = (groups, n, tiles, slots, rows_all, width)
    return pl.pallas_call(
        functools.partial(kernel, dims),
        out_shape=jax.ShapeDtypeStruct((tiles, rows_all, width), jnp.float32),
        in_specs=[
            pl.BlockSpec(memory_space=pl.ANY),
            pl.BlockSpec(memory_space=pl.ANY),
            pl.BlockSpec(memory_space=pl.ANY),
            pl.BlockSpec(memory_space=pltpu.SMEM),
        ],
        out_specs=pl.BlockSpec(memory_space=pl.ANY),
        scratch_shapes=scratch,
        compiler_params=pltpu.CompilerParams(collective_id=0, has_side_effects=True),
        name="ladder",
    )(amplitudes, integrals, task_tiles.T, task_count)


def solution(mesh):
    return jax.shard_map(
        shards,
        mesh=mesh,
        in_specs=(
            P(("task", "own"), None, None),
            P(("task", "own"), None, None),
            P(("task", "own"), None),
            P(("task", "own")),
        ),
        out_specs=P(("task", "own"), None, None),
        check_vma=False,
    )
```

```python
import functools

import jax
import jax.numpy as jnp
from jax import lax
from jax.experimental import pallas as pl
from jax.experimental.pallas import tpu as pltpu
from jax.sharding import PartitionSpec as P

MESH = pl.DeviceIdType.MESH
SHARES = (8, 8, 8)
VIA_Y = (0, 1)
AHEAD = 2
ORDER = "Y0 N0 Y1 N1 Y2 M0 K0 M1 X0 K1 N2 X1 K2 X2 L0 L1 L2 F0 F1 F2"
LEVELS = 32767.0
TINY = 1e-33


def row_chunks(rows_all):
    sizes = [share * rows_all // sum(SHARES) for share in SHARES]
    return [(sum(sizes[:c]), size) for c, size in enumerate(sizes)]


def kernel(dims, amp, integ, lists_hbm, count, out, *scratch):
    groups, n, tiles, slots, rows_all, width = dims
    half = n // 2
    per_owner = slots // n
    chunks = row_chunks(rows_all)
    CHUNKS = len(chunks)
    wide = tiles * width
    group_tiles = n * tiles
    gath = scratch[:CHUNKS]
    (vbuf, weights, psend, precv, pown, qsend, qrecv, ssend, srecv, result, lists, following, source,
     local_sem, v_sem, list_sem, out_sem, sy, ry, sn, rn, ss, rs, st, rt, sv, rv, sp, rp, sq, rq, sc, rc) = scratch[CHUNKS:]

    g = lax.axis_index("task")
    me = lax.axis_index("own")
    core = lax.rem(me, 2)
    y = lax.div(me, 2)
    next_g = lax.rem(g + 1, groups)
    prev_g = lax.rem(g + groups - 1, groups)
    sibling = y * 2 + 1 - core
    to_sibling = {"task": g, "own": sibling}
    to_next = {"task": next_g, "own": me}

    def ahead(d):
        return lax.rem(y + d, half) * 2 + core

    def behind(d):
        return lax.rem(y + half - d, half) * 2 + core

    list_copy = pltpu.make_async_copy(lists_hbm, lists, list_sem)
    list_copy.start()
    barrier = pltpu.get_barrier_semaphore()
    for d in range(1, half):
        pl.semaphore_signal(barrier, inc=1, device_id={"task": g, "own": ahead(d)}, device_id_type=MESH)
    pl.semaphore_signal(barrier, inc=1, device_id=to_sibling, device_id_type=MESH)
    pl.semaphore_signal(barrier, inc=1, device_id={"task": prev_g, "own": me}, device_id_type=MESH)

    v_copy = pltpu.make_async_copy(integ, vbuf, v_sem)
    v_copy.start()
    local = []

    def own_rows(c):
        return amp.at[:, pl.ds(*chunks[c]), :]

    def slot(c, offset, owner):
        return gath[c].at[pl.ds((offset * n + owner) * tiles, tiles)]

    for c in range(CHUNKS):
        copy = pltpu.make_async_copy(own_rows(c), slot(c, 0, me), local_sem.at[c])
        copy.start()
        local.append(copy)

    sends, stored = [], []

    def remote(src, dst, send_sem, recv_sem, device):
        copy = pltpu.make_async_remote_copy(
            src_ref=src, dst_ref=dst, send_sem=send_sem, recv_sem=recv_sem, device_id=device, device_id_type=MESH
        )
        copy.start()
        sends.append(copy)

    def arrived(dst, recv_sem):
        pltpu.make_async_copy(dst, dst, recv_sem).wait()

    pl.semaphore_wait(barrier, half + 1)

    def send_y(c):
        for d in range(1, half):
            remote(own_rows(c), slot(c, 0, me), sy.at[c, d - 1], ry.at[c, d - 1], {"task": g, "own": ahead(d)})

    def send_next(c):
        remote(own_rows(c), slot(c, 1, me), sn.at[c, 0], rn.at[c, 0], to_next)

    def send_sibling(c):
        remote(own_rows(c), slot(c, 0, me), ss.at[c, 0], rs.at[c, 0], to_sibling)

    for c in range(CHUNKS):
        send_y(c)
        if c < AHEAD:
            send_next(c)
        send_sibling(c)

    def relay_y(c):
        for d in range(1, half):
            here = slot(c, 0, behind(d))
            arrived(here, ry.at[c, d - 1])
            if c not in VIA_Y:
                remote(here, slot(c, 1, behind(d)), sn.at[c, d], rn.at[c, d], to_next)
            remote(here, slot(c, 0, behind(d)), ss.at[c, d], rs.at[c, d], to_sibling)
        if c + AHEAD < CHUNKS:
            send_next(c + AHEAD)

    def relay_next(c):
        for d in range(1 if c in VIA_Y else half):
            here = slot(c, 1, behind(d))
            arrived(here, rn.at[c, d])
            if c in VIA_Y:
                for far in range(1, half):
                    remote(here, here, sv.at[c, far - 1], rv.at[c, far - 1], {"task": g, "own": ahead(far)})
            remote(here, here, st.at[c, d], rt.at[c, d], to_sibling)

    def relay_across(c):
        for d in range(1, half):
            here = slot(c, 1, behind(d))
            arrived(here, rv.at[c, d - 1])
            remote(here, here, st.at[c, d], rt.at[c, d], to_sibling)

    list_copy.wait()
    for o in range(n):
        following[slots * n + o] = 0

    def back(step, firsts):
        k = slots - 1 - step
        owner = lax.div(lists[2, k], tiles)
        fresh = []
        for o in range(n):
            first = jnp.where(owner == o, k, firsts[o])
            following[k * n + o] = first
            fresh.append(first)
        return tuple(fresh)

    lax.fori_loop(0, slots, back, tuple(jnp.int32(0) for _ in range(n)))
    v_copy.wait()
    live_slots = count[0]

    def weigh(o, carry):
        k = following[o]
        for j in range(per_owner):
            block = vbuf[k]
            target = lax.rem(lists[2, k], tiles)
            source[o * per_owner + j] = lists[0, k] * group_tiles + lists[1, k]
            for t in range(tiles):
                keep = jnp.logical_and(target == t, k < live_slots)
                weights[o, j * width:(j + 1) * width, t * width:(t + 1) * width] = jnp.where(
                    keep, block, jnp.zeros_like(block)
                )
            k = following[(k + 1) * n + o]
        return carry

    lax.fori_loop(0, n, weigh, 0)

    def product(c, o):
        total = jnp.zeros((chunks[c][1], wide), jnp.float32)
        for j in range(0, per_owner, 2):
            left = gath[c][source[o * per_owner + j]]
            right = gath[c][source[o * per_owner + j + 1]]
            total = total + jnp.dot(
                jnp.concatenate([left, right], -1),
                weights[o, j * width:(j + 2) * width, :],
                preferred_element_type=jnp.float32,
            )
        return total

    def compute(c):
        local[c].wait()
        for d in range(half):
            other = lax.rem(y + half - d, half) * 2 + 1 - core
            arrived(slot(c, 0, other), rs.at[c, d])
            arrived(slot(c, 1, other), rt.at[c, d])
        for d in range(half - 1):
            pair(c, d)

    def pair(c, d):
        mine = pl.ds(*chunks[c])
        psend[d, mine, :] = product(c, lax.rem(y + d + 1, half) * 2 + 1 - core)
        remote(psend.at[d, mine], precv.at[d, mine], sp.at[c, d], rp.at[c, d], to_sibling)
        pown[d, mine, :] = product(c, lax.rem(y + d + 1, half) * 2 + core)

    def compute_kept(c):
        pair(c, half - 1)

    def exchange(c):
        mine = pl.ds(*chunks[c])
        for d in range(half - 1):
            arrived(precv.at[d, mine], rp.at[c, d])
            total = pown[d, mine, :] + precv[d, mine, :]
            top = jnp.maximum(jnp.max(jnp.abs(total), axis=0, keepdims=True), TINY)
            qsend[d, mine, :] = jnp.round(total * (LEVELS / top)).astype(jnp.int32).astype(jnp.int16)
            ssend[c, d] = jnp.broadcast_to(top * (1.0 / LEVELS), (8, wide))
            device = {"task": g, "own": ahead(d + 1)}
            remote(qsend.at[d, mine], qrecv.at[d, mine], sq.at[c, d], rq.at[c, d], device)
            remote(ssend.at[c, d], srecv.at[c, d], sc.at[c, d], rc.at[c, d], device)

    def finish(c):
        mine = pl.ds(*chunks[c])
        arrived(precv.at[half - 1, mine], rp.at[c, half - 1])
        total = pown[half - 1, mine, :] + precv[half - 1, mine, :]
        for d in range(half - 1):
            arrived(qrecv.at[d, mine], rq.at[c, d])
            arrived(srecv.at[c, d], rc.at[c, d])
            total = total + qrecv[d, mine, :].astype(jnp.int32).astype(jnp.float32) * srecv[c, d][0:1]
        for t in range(tiles):
            result[t, mine, :] = total[:, t * width:(t + 1) * width]
        copy = pltpu.make_async_copy(result.at[:, mine, :], out.at[:, mine, :], out_sem.at[c])
        copy.start()
        stored.append(copy)

    stages = {"Y": relay_y, "N": relay_next, "M": relay_across, "K": compute, "L": compute_kept, "X": exchange, "F": finish}
    for word in ORDER.split():
        stages[word[0]](int(word[1:]))
    for copy in sends:
        copy.wait_send()
    for copy in stored:
        copy.wait()


def shards(amplitudes, integrals, task_tiles, task_count):
    tiles, rows_all, width = amplitudes.shape
    slots = integrals.shape[0]
    groups, n = lax.axis_size("task"), lax.axis_size("own")
    half = n // 2
    chunks = row_chunks(rows_all)
    CHUNKS = len(chunks)
    wide = tiles * width
    dma = pltpu.SemaphoreType.DMA
    peers = half - 1
    scratch = [pltpu.VMEM((2 * n * tiles, size, width), amplitudes.dtype) for _, size in chunks]
    scratch += [
        pltpu.VMEM(integrals.shape, integrals.dtype),
        pltpu.VMEM((n, slots // n * width, wide), integrals.dtype),
        pltpu.VMEM((half, rows_all, wide), jnp.float32),
        pltpu.VMEM((half, rows_all, wide), jnp.float32),
        pltpu.VMEM((half, rows_all, wide), jnp.float32),
        pltpu.VMEM((peers, rows_all, wide), jnp.int16),
        pltpu.VMEM((peers, rows_all, wide), jnp.int16),
        pltpu.VMEM((CHUNKS, peers, 8, wide), jnp.float32),
        pltpu.VMEM((CHUNKS, peers, 8, wide), jnp.float32),
        pltpu.VMEM((tiles, rows_all, width), jnp.float32),
        pltpu.SMEM((3, slots), jnp.int32),
        pltpu.SMEM(((slots + 1) * n,), jnp.int32),
        pltpu.SMEM((slots,), jnp.int32),
        dma((CHUNKS,)),
        dma,
        dma,
        dma((CHUNKS,)),
        dma((CHUNKS, peers)), dma((CHUNKS, peers)),
        dma((CHUNKS, half)), dma((CHUNKS, half)),
        dma((CHUNKS, half)), dma((CHUNKS, half)),
        dma((CHUNKS, half)), dma((CHUNKS, half)),
        dma((CHUNKS, peers)), dma((CHUNKS, peers)),
        dma((CHUNKS, half)), dma((CHUNKS, half)),
        dma((CHUNKS, peers)), dma((CHUNKS, peers)),
        dma((CHUNKS, peers)), dma((CHUNKS, peers)),
    ]
    dims = (groups, n, tiles, slots, rows_all, width)
    return pl.pallas_call(
        functools.partial(kernel, dims),
        out_shape=jax.ShapeDtypeStruct((tiles, rows_all, width), jnp.float32),
        in_specs=[
            pl.BlockSpec(memory_space=pl.ANY),
            pl.BlockSpec(memory_space=pl.ANY),
            pl.BlockSpec(memory_space=pl.ANY),
            pl.BlockSpec(memory_space=pltpu.SMEM),
        ],
        out_specs=pl.BlockSpec(memory_space=pl.ANY),
        scratch_shapes=scratch,
        compiler_params=pltpu.CompilerParams(collective_id=0, has_side_effects=True),
        name="ladder",
    )(amplitudes, integrals, task_tiles.T, task_count)


def solution(mesh):
    return jax.shard_map(
        shards,
        mesh=mesh,
        in_specs=(
            P(("task", "own"), None, None),
            P(("task", "own"), None, None),
            P(("task", "own"), None),
            P(("task", "own")),
        ),
        out_specs=P(("task", "own"), None, None),
        check_vma=False,
    )
```
